512 devices in a mesh: phase: 4 (over x), dp: 16 (over z), mp: 8 (over y, core).
Axes of the slice: x: 4, y: 4, z: 16, core: 2. Of those that a mesh axis runs over, the one named last changes fastest.
Arguments:
- text_rows: bfloat16 [2048, 4096], P('dp', 'mp'), may hold values from -6 to 6
- image_rows: bfloat16 [32, 128, 1280], P('dp', ('phase', 'mp')), may hold values from -6 to 6
- tile_counts: int32 [32], P('dp'), may hold values from 1 to 4
- text_lengths: int32 [32], P('dp'), may hold values from 1 to 64
- sample_image: int32 [32], P('dp'), may hold values from 0 to 1
- norm_gain: float32 [4, 4096], P('phase'), may hold values from 0.5 to 2
- query_weight: bfloat16 [4, 4096, 4096], P('phase', 'dp', 'mp'), may hold values from -0.09375 to 0.09375
- keyval_weight: bfloat16 [4, 1280, 8, 256], P('phase', None, 'mp'), may hold values from -0.15625 to 0.15625
- output_weight: bfloat16 [4, 4096, 4096], P('phase', 'dp', 'mp'), may hold values from -0.09375 to 0.09375
- cross_gate: float32 [4], P('phase'), may hold values from -1.5 to 1.5
Outputs:
- section_states: bfloat16 [4, 2048, 4096], P('phase', 'dp', 'mp')
The draws below stay inside these ranges and needn't reach their ends.
All inputs are finite; a program needn't handle non-finite values.
Results may differ from the reference program's by a relative error of at most 0.014.
Values may be sent and summed in bfloat16 or wider, within the bound.
A program may use at most 64 MiB of HBM per device.

```python
import math
import jax
import jax.numpy as jnp
from jax import lax

D = 4096
HD = 128
HQ_DEV = 4
VD = 1280
TROWS = 32
MAXT = 4
SAMP = 2
TXT = 64
KVH = 8
HQ = 32
SECTIONS = 4
IMGS = 32
TOKENS = 2048


def touch_ends(result, own_key, least, high):
    dims = result.shape
    index_at = [jax.random.randint(jax.random.fold_in(own_key, axis), (), 0, dims[axis]) for axis in range(len(dims))]
    result = result.at[tuple(index_at)].set(least)
    longest = dims.index(max(dims))
    index_at[longest] = (index_at[longest] + 1) % dims[longest]
    return result.at[tuple(index_at)].set(high)


def level_of(own_key, shape, split, low, high):
    def one(dim, blocks):
        steps = jax.random.uniform(jax.random.fold_in(jax.random.fold_in(own_key, 6), dim), (blocks,), jnp.float32, low / len(split), high / len(split))
        return jnp.repeat(jnp.exp(steps), shape[dim] // blocks).reshape((-1,) + (1,) * (len(shape) - dim - 1))

    factor_of = one(*split[0])
    for cut in split[1:]:
        factor_of = factor_of * one(*cut)
    return factor_of


def centred(stream_key, shape, spread, reach, shards=(), kind=jnp.bfloat16):
    drawn = spread * jax.random.normal(stream_key, shape, jnp.float32)
    if shards:
        drawn = drawn * level_of(stream_key, shape, shards, -0.22, 0.18)
    return jnp.clip(drawn, -reach, reach).astype(kind)


def setup_inputs(seed: int = 0) -> dict:
    key_of = jax.random.split(jax.random.key(seed), 11)
    text_rows = centred(key_of[0], (TOKENS, D), 1.0, 6.0, ((0, 16), (1, 8)))
    image_rows = centred(key_of[1], (IMGS, MAXT * TROWS, VD), 1.0, 6.0, ((0, 16), (1, 32)))
    tile_counts = touch_ends(jax.random.randint(key_of[2], (IMGS,), 1, MAXT + 1), jax.random.fold_in(key_of[2], 1), 1, MAXT).astype(jnp.int32)
    text_lengths = touch_ends(jax.random.randint(key_of[3], (IMGS,), 1, TXT + 1), jax.random.fold_in(key_of[3], 1), 1, TXT).astype(jnp.int32)
    sample_image = touch_ends(jax.random.randint(key_of[4], (IMGS,), 0, SAMP), jax.random.fold_in(key_of[4], 1), 0, SAMP - 1).astype(jnp.int32)
    norm_gain = jnp.clip(jnp.exp(math.log(2.0) - 1.3862944 * jax.random.uniform(key_of[5], (SECTIONS, D), jnp.float32) ** level_of(key_of[5], (SECTIONS, D), ((0, 4),), -0.2, 0.2)), 0.5, 2.0)
    query_weight = centred(key_of[6], (SECTIONS, D, HQ * HD), D ** -0.5, 0.09375, ((0, 4), (1, 16), (2, 8)))
    keyval_weight = centred(key_of[7], (SECTIONS, VD, KVH, 2 * HD), VD ** -0.5, 0.15625, ((0, 4), (2, 8)))
    output_weight = centred(key_of[8], (SECTIONS, HQ * HD, D), (HQ * HD) ** -0.5, 0.09375, ((0, 4), (1, 16), (2, 8)))
    cross_gate = jnp.clip(jax.random.uniform(key_of[9], (SECTIONS,), jnp.float32, -1.5, 1.5) * level_of(key_of[9], (SECTIONS,), ((0, 4),), -0.4, 0.0), -1.5, 1.5)
    return dict(text_rows=text_rows, image_rows=image_rows, tile_counts=tile_counts, text_lengths=text_lengths, sample_image=sample_image, norm_gain=norm_gain, query_weight=query_weight, keyval_weight=keyval_weight, output_weight=output_weight, cross_gate=cross_gate)


epsilon = 1e-05

def attend(operands):
    queries, keyval, allowed = operands
    key_part = jnp.repeat(keyval[..., :HD], HQ_DEV, axis=1).astype(jnp.float32)
    value_part = jnp.repeat(keyval[..., HD:], HQ_DEV, axis=1).astype(jnp.float32)
    scores = jnp.einsum('rhd,khd->hrk', queries.astype(jnp.float32), key_part) * float(HD) ** (-0.5)
    weighted = jnp.exp(scores) * allowed[None]
    weights = (weighted / lax.optimization_barrier(jnp.sum(weighted, axis=-1, keepdims=True))).astype(jnp.bfloat16)
    context = jnp.einsum('hrk,khd->rhd', weights.astype(jnp.float32), value_part).astype(jnp.bfloat16)
    return context.reshape(queries.shape[0], -1)

def reference(text_rows, image_rows, tile_counts, text_lengths, sample_image, norm_gain, query_weight, keyval_weight, output_weight, cross_gate):
    owners = IMGS // SAMP
    own_rows = SAMP * TXT
    key_count = MAXT * TROWS
    positions = jnp.arange(TOKENS, dtype=jnp.int32)
    live = (positions % TXT < jnp.repeat(text_lengths, TXT)).astype(jnp.float32)
    key_index = jnp.arange(SAMP * key_count, dtype=jnp.int32)
    key_image = key_index // key_count
    tiles_own = tile_counts.reshape(owners, SAMP)
    key_valid = (key_index % key_count)[None, :] < tiles_own[:, key_image] * TROWS
    row_sample = jnp.arange(own_rows, dtype=jnp.int32) // TXT
    row_image = sample_image.reshape(owners, SAMP)[:, row_sample]
    allowed = ((row_image[:, :, None] == key_image[None, None, :]) & key_valid[:, None, :]).astype(jnp.float32)
    carried = text_rows
    states = []
    for section in range(SECTIONS):
        widened = carried.astype(jnp.float32)
        mean_square = lax.optimization_barrier(jnp.mean(widened * widened, axis=-1, keepdims=True))
        normed = (widened * lax.rsqrt(mean_square + epsilon) * norm_gain[section]).astype(jnp.bfloat16)
        queries = jnp.dot(normed, query_weight[section], preferred_element_type=jnp.float32).astype(jnp.bfloat16)
        keyval = jnp.dot(image_rows.reshape(-1, VD), keyval_weight[section].reshape(VD, -1), preferred_element_type=jnp.float32).astype(jnp.bfloat16)
        keyval = keyval.reshape(owners, SAMP * key_count, KVH, 2 * HD)
        context = lax.map(attend, (queries.reshape(owners, own_rows, HQ, HD), keyval, allowed))
        attended = jnp.dot(context.reshape(TOKENS, HQ * HD), output_weight[section], preferred_element_type=jnp.float32)
        carried = (carried.astype(jnp.float32) + live[:, None] * jnp.tanh(cross_gate[section]) * attended).astype(jnp.bfloat16)
        states.append(carried)
    return jnp.stack(states)
```

```python
import functools

import jax
import jax.numpy as jnp
from jax import lax
from jax.experimental import pallas as pl
from jax.experimental.pallas import tpu as pltpu
from jax.sharding import PartitionSpec as P

MESH = pl.DeviceIdType.MESH
HD = 128
TROWS = 32
SAMP = 2
SUBS = 2
PARTS = 9

epsilon = 1e-05


def kernel(
    sizes,
    tiles_ref,
    lengths_ref,
    pick_ref,
    gate_ref,
    x_in,
    image_in,
    gain_ref,
    wq_in,
    wkv_ref,
    wo_in,
    out_ref,
    wq_buf,
    wo_buf,
    x_buf,
    ctx_buf,
    image_buf,
    kv_buf,
    acc,
    local_sem,
    ring_send,
    ring_recv,
    spread_send,
    spread_recv,
    image_send,
    image_recv,
    hop_send,
    hop_recv,
):
    phases, ring, groups = sizes
    phase = lax.axis_index("phase")
    d = lax.axis_index("dp")
    m = lax.axis_index("mp")
    rows, width = x_in.shape
    half_rows = rows // SAMP
    depth = wq_in.shape[0]
    sub = depth // SUBS
    steps = ring // 2
    first = phase == 0

    up, down = lax.rem(d + 1, ring), lax.rem(d + ring - 1, ring)
    sibling = m + 1 - 2 * lax.rem(m, 2)
    right, left = lax.rem(m + 2, groups), lax.rem(m + groups - 2, groups)
    across = lax.rem(m + 4, groups)

    def twin(slot):
        return slot + 1 - 2 * lax.rem(slot, 2)

    own_wq = pltpu.make_async_copy(
        wq_in, wq_buf.at[pl.ds(pl.multiple_of(d * depth, depth), depth), :], local_sem.at[0]
    )
    own_wo = pltpu.make_async_copy(
        wo_in, wo_buf.at[pl.ds(pl.multiple_of(d * depth, depth), depth), :], local_sem.at[1]
    )
    piece = image_in.shape[0]
    place = phase * groups + m
    own_image = pltpu.make_async_copy(
        image_in, image_buf.at[pl.ds(pl.multiple_of(place * piece, piece), piece), :], local_sem.at[2]
    )
    own_x = pltpu.make_async_copy(x_in, x_buf.at[m], local_sem.at[3])
    own_wq.start()
    own_wo.start()
    own_image.start()

    @pl.when(first)
    def _():
        own_x.start()

    barrier = pltpu.get_barrier_semaphore()
    for target in (up, down):
        pl.semaphore_signal(barrier, inc=1, device_id={"dp": target}, device_id_type=MESH)
    for k in range(1, groups):
        pl.semaphore_signal(
            barrier, inc=1, device_id={"mp": lax.rem(m + k, groups)}, device_id_type=MESH
        )
    for k in range(1, phases):
        pl.semaphore_signal(
            barrier, inc=1, device_id={"phase": lax.rem(phase + k, phases)}, device_id_type=MESH
        )
    own_wq.wait()
    own_wo.wait()
    own_image.wait()

    @pl.when(first)
    def _():
        own_x.wait()

    pl.semaphore_wait(barrier, 2 + groups - 1 + phases - 1)

    def ring_copy(mat, s, u, way, incoming=False):
        shift = s + 1 if incoming else s
        block = lax.rem(d + (ring - shift if way == 0 else shift), ring)
        at = pl.ds(pl.multiple_of(block * depth + u * sub, sub), sub)
        buf = (wq_buf, wo_buf)[mat].at[at, :]
        index = (((mat * 2 + way) * steps) + s) * SUBS + u
        return pltpu.make_async_remote_copy(
            src_ref=buf,
            dst_ref=buf,
            send_sem=ring_send.at[index],
            recv_sem=ring_recv.at[index],
            device_id={"dp": up if way == 0 else down},
            device_id_type=MESH,
        )

    def used(s, u, way):
        return s < steps - 1 or (u < SUBS // 2) == (way == 0)

    def ring_step(mat, s):
        for u in range(SUBS):
            for way in range(2):
                if used(s, u, way):
                    if s > 0:
                        ring_copy(mat, s - 1, u, way, True).wait_recv()
                    ring_copy(mat, s, u, way).start()

    def ring_end(mat):
        for u in range(SUBS):
            for way in range(2):
                last = steps - 1 if used(steps - 1, u, way) else steps - 2
                ring_copy(mat, last, u, way, True).wait_recv()

    def ring_sent(mat):
        for s in range(steps):
            for u in range(SUBS):
                for way in range(2):
                    if used(s, u, way):
                        ring_copy(mat, s, u, way).wait_send()

    def image_copy(k, incoming=False):
        owner = lax.rem(m + groups - k, groups) if incoming else m
        at = pl.ds(pl.multiple_of((phase * groups + owner) * piece, piece), piece)
        return pltpu.make_async_remote_copy(
            src_ref=image_buf.at[at, :],
            dst_ref=image_buf.at[at, :],
            send_sem=image_send.at[k],
            recv_sem=image_recv.at[k],
            device_id={"mp": lax.rem(m + k, groups)},
            device_id_type=MESH,
        )

    def image_block_copy(k, incoming=False):
        owner = lax.rem(phase + phases - k, phases) if incoming else phase
        span = groups * piece
        at = pl.ds(pl.multiple_of(owner * span, span), span)
        return pltpu.make_async_remote_copy(
            src_ref=image_buf.at[at, :],
            dst_ref=image_buf.at[at, :],
            send_sem=image_send.at[groups + k],
            recv_sem=image_recv.at[groups + k],
            device_id={"phase": lax.rem(phase + k, phases)},
            device_id_type=MESH,
        )

    def spread_copy(which, h, part, incoming=False):
        buf = (x_buf, ctx_buf)[which]
        start, count = h * half_rows, half_rows
        quarter = half_rows // 2
        target = sibling
        if part == 0:
            slot = sibling if incoming else m
        elif part == 1:
            slot, target = (left if incoming else m), right
        elif part == 2:
            slot, target = (right if incoming else m), left
        elif part == 3:
            slot = twin(left) if incoming else left
        elif part == 4:
            slot = twin(right) if incoming else right
        elif part == 5:
            slot, target, count = (across if incoming else left), right, quarter
        elif part == 6:
            slot, target, count = (across if incoming else right), left, quarter
            start += quarter
        elif part == 7:
            slot, count = (twin(across) if incoming else across), quarter
        else:
            slot, count = (twin(across) if incoming else across), quarter
            start += quarter
        ref = buf.at[slot, pl.ds(start, count), :]
        index = (which * SAMP + h) * PARTS + part
        return pltpu.make_async_remote_copy(
            src_ref=ref,
            dst_ref=ref,
            send_sem=spread_send.at[index],
            recv_sem=spread_recv.at[index],
            device_id={"mp": target},
            device_id_type=MESH,
        )

    def spread_open(which, h):
        for part in (1, 2, 0):
            spread_copy(which, h, part).start()

    def spread_pass(which, h):
        spread_copy(which, h, 1, True).wait_recv()
        spread_copy(which, h, 5).start()
        spread_copy(which, h, 3).start()
        spread_copy(which, h, 2, True).wait_recv()
        spread_copy(which, h, 6).start()
        spread_copy(which, h, 4).start()

    def spread_far(which, h):
        for part in (5, 6):
            spread_copy(which, h, part, True).wait_recv()
            spread_copy(which, h, part + 2).start()

    def spread_sent(which, h):
        for part in range(PARTS):
            spread_copy(which, h, part).wait_send()

    def hop_copy(h):
        at = pl.ds(h * half_rows, half_rows)
        return pltpu.make_async_remote_copy(
            src_ref=out_ref.at[at, :],
            dst_ref=x_buf.at[m, at, :],
            send_sem=hop_send.at[h],
            recv_sem=hop_recv.at[h],
            device_id={"phase": lax.rem(phase + 1, phases)},
            device_id_type=MESH,
        )

    def make_keyval():
        kv_buf[...] = jnp.dot(
            image_buf[...], wkv_ref[...], preferred_element_type=jnp.float32
        ).astype(jnp.bfloat16)

    def column(slot):
        return pl.ds(pl.multiple_of(slot * width, width), width)

    def query_term(h, slot, squares, begin=False):
        at = pl.ds(h * half_rows, half_rows)
        wide = x_buf[slot, at, :].astype(jnp.float32)
        scaled = (wide * gain_ref[:, column(slot)]).astype(jnp.bfloat16)
        term = jnp.dot(scaled, wq_buf[column(slot), :], preferred_element_type=jnp.float32)
        if begin:
            acc[at, :] = term
        else:
            acc[at, :] += term
        part = jnp.sum(wide * wide, axis=-1, keepdims=True)
        return part if squares is None else squares + part

    def attend(h, squares):
        at = pl.ds(h * half_rows, half_rows)
        factor = lax.rsqrt(squares / (width * groups) + epsilon)
        queries = (acc[at, :] * factor).astype(jnp.bfloat16)
        count = kv_buf.shape[0]
        key = lax.broadcasted_iota(jnp.int32, (half_rows, count), 1)
        per = piece // SAMP
        image = (key // per) % SAMP
        row = (key // piece) * per + key % per
        limit = jnp.where(image == 0, tiles_ref[0], tiles_ref[1]) * TROWS
        allowed = ((row < limit) & (image == pick_ref[h])).astype(jnp.float32)
        for g in range(width // HD):
            cols = slice(g * HD, (g + 1) * HD)
            scores = lax.dot_general(
                queries[:, cols],
                kv_buf[:, :HD],
                (((1,), (1,)), ((), ())),
                preferred_element_type=jnp.float32,
            ) * (float(HD) ** (-0.5))
            prob = jnp.exp(scores) * allowed
            weights = (prob / jnp.sum(prob, axis=-1, keepdims=True)).astype(jnp.bfloat16)
            ctx_buf[m, at, cols] = jnp.dot(
                weights, kv_buf[:, HD:], preferred_element_type=jnp.float32
            ).astype(jnp.bfloat16)

    def out_term(h, slot, begin=False):
        at = pl.ds(h * half_rows, half_rows)
        term = jnp.dot(
            ctx_buf[slot, at, :], wo_buf[column(slot), :], preferred_element_type=jnp.float32
        )
        if begin:
            acc[at, :] = term
        else:
            acc[at, :] += term

    def finish(h):
        at = pl.ds(h * half_rows, half_rows)
        position = lax.broadcasted_iota(jnp.int32, (half_rows, width), 0)
        gate = jnp.tanh(jnp.full((half_rows, width), gate_ref[0], jnp.float32))
        moved = jnp.where(position < lengths_ref[h], gate * acc[at, :], 0.0)
        out_ref[at, :] = (x_buf[m, at, :].astype(jnp.float32) + moved).astype(jnp.bfloat16)

        @pl.when(phase < phases - 1)
        def _():
            hop_copy(h).start()

    def query_rest(h, squares):
        spread_copy(0, h, 0, True).wait_recv()
        squares = query_term(h, sibling, squares)
        squares = query_term(h, left, squares)
        squares = query_term(h, right, squares)
        spread_copy(0, h, 3, True).wait_recv()
        squares = query_term(h, twin(left), squares)
        spread_copy(0, h, 4, True).wait_recv()
        squares = query_term(h, twin(right), squares)
        squares = query_term(h, across, squares)
        for part in (7, 8):
            spread_copy(0, h, part, True).wait_recv()
        return query_term(h, twin(across), squares)

    def out_rest(h):
        spread_copy(1, h, 0, True).wait_recv()
        out_term(h, sibling)
        out_term(h, left)
        out_term(h, right)
        spread_copy(1, h, 3, True).wait_recv()
        out_term(h, twin(left))
        spread_copy(1, h, 4, True).wait_recv()
        out_term(h, twin(right))
        out_term(h, across)
        for part in (7, 8):
            spread_copy(1, h, part, True).wait_recv()
        out_term(h, twin(across))

    halves = range(SAMP)

    ring_step(0, 0)
    for k in range(1, groups):
        image_copy(k).start()

    @pl.when(first)
    def _():
        for h in halves:
            spread_open(0, h)

    for k in range(1, groups):
        image_copy(k, True).wait_recv()
    for k in range(1, phases):
        image_block_copy(k).start()

    @pl.when(first)
    def _():
        for h in halves:
            spread_pass(0, h)

    ring_step(0, 1)

    @pl.when(first)
    def _():
        for h in halves:
            spread_far(0, h)

    ring_step(0, 2)
    ring_step(0, 3)
    for k in range(1, phases):
        image_block_copy(k, True).wait_recv()
    make_keyval()
    for s in range(4, steps):
        ring_step(0, s)
    ring_step(1, 0)
    ring_end(0)

    @pl.when(first)
    def _():
        for h in halves:
            attend(h, query_rest(h, query_term(h, m, None, True)))
            spread_open(1, h)

    ring_step(1, 1)

    @pl.when(first)
    def _():
        for h in halves:
            spread_pass(1, h)

    ring_step(1, 2)
    ring_step(1, 3)

    @pl.when(first)
    def _():
        for h in halves:
            spread_far(1, h)

    for s in range(4, steps):
        ring_step(1, s)
    ring_end(1)

    @pl.when(first)
    def _():
        for h in halves:
            out_term(h, m, True)
            out_rest(h)
            finish(h)

    @pl.when(phase > 0)
    def _():
        for h in halves:
            hop_copy(h).wait_recv()
            spread_open(0, h)
        for h in halves:
            squares = query_term(h, m, None, True)
            spread_pass(0, h)
            spread_far(0, h)
            attend(h, query_rest(h, squares))
            spread_open(1, h)
        for h in halves:
            out_term(h, m, True)
            spread_pass(1, h)
            spread_far(1, h)
            out_rest(h)
            finish(h)

    for mat in range(2):
        ring_sent(mat)
    for k in range(1, groups):
        image_copy(k).wait_send()
    for k in range(1, phases):
        image_block_copy(k).wait_send()
    for which in range(2):
        for h in halves:
            spread_sent(which, h)

    @pl.when(phase < phases - 1)
    def _():
        for h in halves:
            hop_copy(h).wait_send()


def solution(mesh):
    sizes = (mesh.shape["phase"], mesh.shape["dp"], mesh.shape["mp"])
    phases, ring, groups = sizes

    def on_device(
        text_rows,
        image_rows,
        tile_counts,
        text_lengths,
        sample_image,
        norm_gain,
        query_weight,
        keyval_weight,
        output_weight,
        cross_gate,
    ):
        rows, width = text_rows.shape
        samples, piece, vision = image_rows.shape
        depth = query_weight.shape[1]
        columns = query_weight.shape[2]
        smem = pl.BlockSpec(memory_space=pltpu.SMEM)
        vmem = pl.BlockSpec(memory_space=pltpu.VMEM)
        anywhere = pl.BlockSpec(memory_space=pl.ANY)
        keys = samples * piece * phases * groups
        ring_copies = 2 * 2 * (ring // 2) * SUBS
        result = pl.pallas_call(
            functools.partial(kernel, sizes),
            out_shape=jax.ShapeDtypeStruct((rows, width), jnp.bfloat16),
            in_specs=[smem] * 4 + [anywhere, anywhere, vmem, anywhere, vmem, anywhere],
            out_specs=vmem,
            scratch_shapes=[
                pltpu.VMEM((ring * depth, columns), jnp.bfloat16),
                pltpu.VMEM((ring * depth, columns), jnp.bfloat16),
                pltpu.VMEM((groups, rows, width), jnp.bfloat16),
                pltpu.VMEM((groups, rows, width), jnp.bfloat16),
                pltpu.VMEM((keys, vision), jnp.bfloat16),
                pltpu.VMEM((keys, 2 * HD), jnp.bfloat16),
                pltpu.VMEM((rows, width), jnp.float32),
                pltpu.SemaphoreType.DMA((4,)),
                pltpu.SemaphoreType.DMA((ring_copies,)),
                pltpu.SemaphoreType.DMA((ring_copies,)),
                pltpu.SemaphoreType.DMA((2 * SAMP * PARTS,)),
                pltpu.SemaphoreType.DMA((2 * SAMP * PARTS,)),
                pltpu.SemaphoreType.DMA((groups + phases,)),
                pltpu.SemaphoreType.DMA((groups + phases,)),
                pltpu.SemaphoreType.DMA((SAMP,)),
                pltpu.SemaphoreType.DMA((SAMP,)),
            ],
            compiler_params=pltpu.CompilerParams(
                collective_id=0, has_side_effects=True, vmem_limit_bytes=40 * 1024 * 1024
            ),
        )(
            tile_counts,
            text_lengths,
            sample_image,
            cross_gate,
            text_rows,
            image_rows.reshape(samples * piece, vision),
            norm_gain,
            query_weight[0],
            keyval_weight[0, :, 0, :],
            output_weight[0],
        )
        return result[None]

    placed = (
        P("dp", "mp"),
        P("dp", ("phase", "mp"), None),
        P("dp"),
        P("dp"),
        P("dp"),
        P("phase", None),
        P("phase", "dp", "mp"),
        P("phase", None, "mp", None),
        P("phase", "dp", "mp"),
        P("phase"),
    )
    return jax.shard_map(
        on_device, mesh=mesh, in_specs=placed, out_specs=P("phase", "dp", "mp"), check_vma=False
    )
```

```python
import functools

import jax
import jax.numpy as jnp
from jax import lax
from jax.experimental import pallas as pl
from jax.experimental.pallas import tpu as pltpu
from jax.sharding import PartitionSpec as P

MESH = pl.DeviceIdType.MESH
HD = 128
TROWS = 32
SAMP = 2
SUBS = 4
CHIPS = 4

epsilon = 1e-05


def kernel(
    sizes,
    tiles_in,
    lengths_in,
    pick_in,
    gate_in,
    x_in,
    image_in,
    gain_in,
    wq_in,
    wkv_in,
    wo_in,
    out_ref,
    tiles_ref,
    lengths_ref,
    pick_ref,
    gate_ref,
    gain_ref,
    wkv_ref,
    wq_buf,
    wo_buf,
    guest_buf,
    x_buf,
    ctx_buf,
    image_buf,
    kv_buf,
    acc,
    local_sem,
    ring_send,
    ring_recv,
    guest_send,
    guest_recv,
    return_send,
    return_recv,
    cross_send,
    cross_recv,
    pair_send,
    pair_recv,
    image_send,
    image_recv,
):
    phases, ring, groups = sizes
    phase = lax.axis_index("phase")
    d = lax.axis_index("dp")
    m = lax.axis_index("mp")
    rows, width = x_in.shape
    half_rows = rows // SAMP
    depth = wq_in.shape[0]
    sub = depth // SUBS
    steps = ring // 2
    heads = width // HD

    up, down = lax.rem(d + 1, ring), lax.rem(d + ring - 1, ring)
    ahead = lax.rem(phase + 1, phases)
    behind = lax.rem(phase + phases - 1, phases)
    sibling = m + 1 - 2 * lax.rem(m, 2)

    def slot_of(j):
        return lax.rem(m + 2 * j, groups)

    def target_of(j):
        return lax.rem(m + groups - 2 * j, groups)

    def twin(slot):
        return slot + 1 - 2 * lax.rem(slot, 2)

    own_rows = pl.ds(pl.multiple_of(d * depth, depth), depth)
    piece = image_in.shape[0]
    place = pl.ds(pl.multiple_of((phase * groups + m) * piece, piece), piece)
    moves = (
        (wq_in, wq_buf.at[own_rows, :]),
        (image_in, image_buf.at[place, :]),
        (wo_in, wo_buf.at[own_rows, :]),
        (gain_in, gain_ref),
        (wkv_in, wkv_ref),
        (tiles_in, tiles_ref),
        (lengths_in, lengths_ref),
        (pick_in, pick_ref),
        (gate_in, gate_ref),
    )
    local = [
        pltpu.make_async_copy(source, target, local_sem.at[i])
        for i, (source, target) in enumerate(moves)
    ]
    for copy in local:
        copy.start()

    barrier = pltpu.get_barrier_semaphore()
    peers = [{"dp": up}, {"dp": down}]
    peers += [{"mp": lax.rem(m + k, groups)} for k in range(1, groups)]
    peers += [{"phase": lax.rem(phase + k, phases)} for k in range(1, phases)]
    peers += [{"phase": ahead, "mp": target_of(j)} for j in range(1, CHIPS)]
    peers += [{"phase": behind, "mp": slot_of(j)} for j in range(1, CHIPS)]
    for peer in peers:
        pl.semaphore_signal(barrier, inc=1, device_id=peer, device_id_type=MESH)
    for copy in local[:3]:
        copy.wait()
    pl.semaphore_wait(barrier, len(peers))

    def lane_on(mat, u):
        if mat == 0 or (mat == 1 and u < SUBS // 2):
            return None
        if mat == 1:
            return phase > (1 if u == SUBS - 1 else 0)
        if u < SUBS // 2:
            return False
        return phase >= (phases - 2 if u == SUBS - 1 else phases - 1)

    def guarded(predicate, move):
        if predicate is None:
            move()
        elif predicate is not False:
            pl.when(predicate)(move)

    def block_rows(s, u, way, incoming):
        shift = s + 1 if incoming else s
        block = lax.rem(d + (ring - shift if way == 0 else shift), ring)
        return pl.ds(pl.multiple_of(block * depth + u * sub, sub), sub)

    def ring_copy(mat, s, u, way, incoming=False):
        buf = (wq_buf, wo_buf, guest_buf)[mat].at[block_rows(s, u, way, incoming), :]
        index = ((mat * 2 + way) * steps + s) * SUBS + u
        return pltpu.make_async_remote_copy(
            src_ref=buf,
            dst_ref=buf,
            send_sem=ring_send.at[index],
            recv_sem=ring_recv.at[index],
            device_id={"dp": up if way == 0 else down},
            device_id_type=MESH,
        )

    mirror = phases - 1 - phase

    def guest_copy(u):
        at = pl.ds(pl.multiple_of(d * depth + u * sub, sub), sub)
        return pltpu.make_async_remote_copy(
            src_ref=wo_buf.at[at, :],
            dst_ref=guest_buf.at[at, :],
            send_sem=guest_send.at[u],
            recv_sem=guest_recv.at[u],
            device_id={"phase": mirror},
            device_id_type=MESH,
        )

    def return_copy(s, u, way):
        at = block_rows(s, u, way, True)
        index = (way * steps + s) * SUBS + u
        return pltpu.make_async_remote_copy(
            src_ref=guest_buf.at[at, :],
            dst_ref=wo_buf.at[at, :],
            send_sem=return_send.at[index],
            recv_sem=return_recv.at[index],
            device_id={"phase": mirror},
            device_id_type=MESH,
        )

    def goes_last(u, way):
        return u % 2 == way

    def ring_open(mat):
        for u in range(SUBS):

            def move(u=u):
                if mat == 2:
                    guest_copy(u).wait_recv()
                for way in range(2):
                    ring_copy(mat, 0, u, way).start()

            guarded(lane_on(mat, u), move)

    def ring_pass(mat, s, u, way, last):
        ring_copy(mat, s - 1, u, way, True).wait_recv()
        if not last:
            ring_copy(mat, s, u, way).start()
        if mat == 2:
            return_copy(s - 1, u, way).start()

    def ring_steps(mat, lo, hi):
        def one(s, carry):
            for u in range(SUBS):

                def move(u=u):
                    ring_pass(mat, s, u, u % 2, False)

                    @pl.when(s < steps - 1)
                    def _():
                        ring_pass(mat, s, u, 1 - u % 2, False)

                guarded(lane_on(mat, u), move)
            return carry

        lax.fori_loop(lo, hi, one, 0)

    def ring_end(mat):
        for u in range(SUBS):

            def move(u=u):
                for way in range(2):
                    ring_pass(mat, steps if goes_last(u, way) else steps - 1, u, way, True)

            guarded(lane_on(mat, u), move)

    def each_lane(predicate_of, act):
        def one(s, carry):
            for u in range(SUBS):

                def move(u=u):
                    act(s, u, u % 2)

                    @pl.when(s < steps - 1)
                    def _():
                        act(s, u, 1 - u % 2)

                guarded(predicate_of(u), move)
            return carry

        lax.fori_loop(0, steps, one, 0)

    def ring_sent(mat):
        each_lane(lambda u: lane_on(mat, u), lambda s, u, way: ring_copy(mat, s, u, way).wait_send())

    def hosted(u):
        if u < SUBS // 2:
            return False
        return phase < (2 if u == SUBS - 1 else 1)

    def image_copy(k, incoming=False):
        owner = lax.rem(m + groups - k, groups) if incoming else m
        at = pl.ds(pl.multiple_of((phase * groups + owner) * piece, piece), piece)
        return pltpu.make_async_remote_copy(
            src_ref=image_buf.at[at, :],
            dst_ref=image_buf.at[at, :],
            send_sem=image_send.at[k],
            recv_sem=image_recv.at[k],
            device_id={"mp": lax.rem(m + k, groups)},
            device_id_type=MESH,
        )

    def image_block_copy(k, incoming=False):
        owner = lax.rem(phase + phases - k, phases) if incoming else phase
        span = groups * piece
        at = pl.ds(pl.multiple_of(owner * span, span), span)
        return pltpu.make_async_remote_copy(
            src_ref=image_buf.at[at, :],
            dst_ref=image_buf.at[at, :],
            send_sem=image_send.at[groups + k],
            recv_sem=image_recv.at[groups + k],
            device_id={"phase": lax.rem(phase + k, phases)},
            device_id_type=MESH,
        )

    def cross_copy(which, h, j, source=None):
        at = pl.ds(h * half_rows, half_rows)
        index = (which * SAMP + h) * CHIPS + j
        target = {"mp": target_of(j)}
        if which == 0:
            target["phase"] = ahead
        dst = (x_buf, ctx_buf)[which].at[m, at, :]
        return pltpu.make_async_remote_copy(
            src_ref=dst if source is None else source.at[at, :],
            dst_ref=dst,
            send_sem=cross_send.at[index],
            recv_sem=cross_recv.at[index],
            device_id=target,
            device_id_type=MESH,
        )

    def pair_copy(which, h, j, incoming=False):
        slot = twin(slot_of(j)) if incoming else slot_of(j)
        ref = (x_buf, ctx_buf)[which].at[slot, pl.ds(h * half_rows, half_rows), :]
        index = (which * SAMP + h) * CHIPS + j
        return pltpu.make_async_remote_copy(
            src_ref=ref,
            dst_ref=ref,
            send_sem=pair_send.at[index],
            recv_sem=pair_recv.at[index],
            device_id={"mp": sibling},
            device_id_type=MESH,
        )

    def send_rows(h, source):
        for j in (2, 1, 3, 0):
            cross_copy(0, h, j, source).start()

    def make_keyval():
        kv_buf[...] = jnp.dot(
            image_buf[...], wkv_ref[...], preferred_element_type=jnp.float32
        ).astype(jnp.bfloat16)

    def column(slot):
        return pl.ds(pl.multiple_of(slot * width, width), width)

    def add(h, term, begin):
        at = pl.ds(h * half_rows, half_rows)
        if begin:
            acc[at, :] = term
        else:
            acc[at, :] += term

    def query_term(h, slot, squares, begin=False):
        wide = x_buf[slot, pl.ds(h * half_rows, half_rows), :].astype(jnp.float32)
        scaled = (wide * gain_ref[:, column(slot)]).astype(jnp.bfloat16)
        add(h, jnp.dot(scaled, wq_buf[column(slot), :], preferred_element_type=jnp.float32), begin)
        part = jnp.sum(wide * wide, axis=-1, keepdims=True)
        return part if begin else squares + part

    def out_term(h, slot, begin=False):
        rows_here = ctx_buf[slot, pl.ds(h * half_rows, half_rows), :]
        add(h, jnp.dot(rows_here, wo_buf[column(slot), :], preferred_element_type=jnp.float32), begin)

    def attend(h, squares):
        at = pl.ds(h * half_rows, half_rows)
        factor = lax.rsqrt(squares / (width * groups) + epsilon)
        queries = (acc[at, :] * factor).astype(jnp.bfloat16)
        stacked = jnp.concatenate([queries[:, g * HD : (g + 1) * HD] for g in range(heads)], axis=0)
        count = kv_buf.shape[0]
        key = lax.broadcasted_iota(jnp.int32, (1, count), 1)
        image = jnp.bitwise_and(jnp.right_shift(key, 2), 1)
        row = jnp.right_shift(key, 3) * 4 + jnp.bitwise_and(key, 3)
        limit = jnp.where(image == 0, tiles_ref[0], tiles_ref[1]) * TROWS
        allowed = ((row < limit) & (image == pick_ref[h])).astype(jnp.float32)
        scores = lax.dot_general(
            stacked, kv_buf[:, :HD], (((1,), (1,)), ((), ())), preferred_element_type=jnp.float32
        ) * (float(HD) ** (-0.5))
        prob = jnp.exp(scores) * allowed
        weights = (prob / jnp.sum(prob, axis=-1, keepdims=True)).astype(jnp.bfloat16)
        context = jnp.dot(weights, kv_buf[:, HD:], preferred_element_type=jnp.float32).astype(
            jnp.bfloat16
        )
        for g in range(heads):
            ctx_buf[m, at, g * HD : (g + 1) * HD] = context[g * half_rows : (g + 1) * half_rows, :]

    def section_front(h):
        squares = None
        for j in (0, 1, 3, 2):
            cross_copy(0, h, j).wait_recv()
            pair_copy(0, h, j).start()
            squares = query_term(h, slot_of(j), squares, begin=j == 0)
        for j in (0, 1, 3, 2):
            pair_copy(0, h, j, True).wait_recv()
            squares = query_term(h, twin(slot_of(j)), squares)
        attend(h, squares)
        for j in (2, 1, 3):
            cross_copy(1, h, j).start()
        pair_copy(1, h, 0).start()

    def section_back(h):
        out_term(h, m, True)
        for j in (1, 3, 2):
            cross_copy(1, h, j).wait_recv()
            pair_copy(1, h, j).start()
            out_term(h, slot_of(j))
        for j in (0, 1, 3, 2):
            pair_copy(1, h, j, True).wait_recv()
            out_term(h, twin(slot_of(j)))
        at = pl.ds(h * half_rows, half_rows)
        position = lax.broadcasted_iota(jnp.int32, (half_rows, width), 0)
        gate = jnp.tanh(jnp.full((1, width), gate_ref[0], jnp.float32))
        moved = jnp.where(position < lengths_ref[h], gate * acc[at, :], 0.0)
        out_ref[at, :] = (x_buf[m, at, :].astype(jnp.float32) + moved).astype(jnp.bfloat16)

        @pl.when(phase < phases - 1)
        def _():
            send_rows(h, out_ref)

    for u in range(SUBS):
        guarded(hosted(u), lambda u=u: guest_copy(u).start())
    ring_open(0)
    for k in range(1, groups):
        image_copy(k).start()

    @pl.when(phase == phases - 1)
    def _():
        for h in range(SAMP):
            send_rows(h, x_in)

    ring_open(2)
    for k in range(1, groups):
        image_copy(k, True).wait_recv()
    for k in range(1, phases):
        image_block_copy(k).start()
    middle = steps // 2
    for s in range(1, middle):
        ring_steps(2, 2 * s - 1, 2 * s)
        ring_steps(0, s, s + 1)
        ring_steps(2, 2 * s, 2 * s + 1)
    for k in range(1, phases):
        image_block_copy(k, True).wait_recv()
    for copy in local[3:]:
        copy.wait()
    make_keyval()
    ring_steps(2, steps - 1, steps)
    ring_steps(0, middle, middle + 1)
    ring_end(2)
    ring_open(1)
    for s in range(middle + 1, steps):
        ring_steps(0, s, s + 1)
        ring_steps(1, s - middle, s - middle + 1)
    ring_end(0)

    others = lax.div(phase + phases - 1, phases)
    pause = middle + (steps - middle) * others
    resume = pause + 1 - others
    ring_steps(1, middle, pause)
    section_front(0)
    ring_steps(1, pause, resume)
    section_front(1)
    ring_steps(1, resume, steps)
    ring_end(1)
    each_lane(hosted, lambda s, u, way: return_copy(s, u, way).wait_recv())
    for h in range(SAMP):
        section_back(h)

    for mat in range(3):
        ring_sent(mat)
    for u in range(SUBS):
        guarded(hosted(u), lambda u=u: guest_copy(u).wait_send())
    each_lane(lambda u: lane_on(2, u), lambda s, u, way: return_copy(s, u, way).wait_send())
    for k in range(1, groups):
        image_copy(k).wait_send()
    for k in range(1, phases):
        image_block_copy(k).wait_send()
    for h in range(SAMP):
        for j in range(CHIPS):
            cross_copy(0, h, j, out_ref).wait_send()
            pair_copy(0, h, j).wait_send()
            pair_copy(1, h, j).wait_send()
            if j:
                cross_copy(1, h, j).wait_send()


def solution(mesh):
    sizes = (mesh.shape["phase"], mesh.shape["dp"], mesh.shape["mp"])
    phases, ring, groups = sizes

    def on_device(
        text_rows,
        image_rows,
        tile_counts,
        text_lengths,
        sample_image,
        norm_gain,
        query_weight,
        keyval_weight,
        output_weight,
        cross_gate,
    ):
        rows, width = text_rows.shape
        samples, piece, vision = image_rows.shape
        depth = query_weight.shape[1]
        columns = query_weight.shape[2]
        vmem = pl.BlockSpec(memory_space=pltpu.VMEM)
        anywhere = pl.BlockSpec(memory_space=pl.ANY)
        keys = samples * piece * phases * groups
        lane_copies = 2 * (ring // 2) * SUBS
        result = pl.pallas_call(
            functools.partial(kernel, sizes),
            out_shape=jax.ShapeDtypeStruct((rows, width), jnp.bfloat16),
            in_specs=[anywhere] * 10,
            out_specs=vmem,
            scratch_shapes=[
                pltpu.SMEM(tile_counts.shape, jnp.int32),
                pltpu.SMEM(text_lengths.shape, jnp.int32),
                pltpu.SMEM(sample_image.shape, jnp.int32),
                pltpu.SMEM(cross_gate.shape, jnp.float32),
                pltpu.VMEM(norm_gain.shape, jnp.float32),
                pltpu.VMEM((vision, 2 * HD), jnp.bfloat16),
                pltpu.VMEM((ring * depth, columns), jnp.bfloat16),
                pltpu.VMEM((ring * depth, columns), jnp.bfloat16),
                pltpu.VMEM((ring * depth, columns), jnp.bfloat16),
                pltpu.VMEM((groups, rows, width), jnp.bfloat16),
                pltpu.VMEM((groups, rows, width), jnp.bfloat16),
                pltpu.VMEM((keys, vision), jnp.bfloat16),
                pltpu.VMEM((keys, 2 * HD), jnp.bfloat16),
                pltpu.VMEM((rows, width), jnp.float32),
                pltpu.SemaphoreType.DMA((9,)),
                pltpu.SemaphoreType.DMA((3 * lane_copies,)),
                pltpu.SemaphoreType.DMA((3 * lane_copies,)),
                pltpu.SemaphoreType.DMA((SUBS,)),
                pltpu.SemaphoreType.DMA((SUBS,)),
                pltpu.SemaphoreType.DMA((lane_copies,)),
                pltpu.SemaphoreType.DMA((lane_copies,)),
                pltpu.SemaphoreType.DMA((2 * SAMP * CHIPS,)),
                pltpu.SemaphoreType.DMA((2 * SAMP * CHIPS,)),
                pltpu.SemaphoreType.DMA((2 * SAMP * CHIPS,)),
                pltpu.SemaphoreType.DMA((2 * SAMP * CHIPS,)),
                pltpu.SemaphoreType.DMA((groups + phases,)),
                pltpu.SemaphoreType.DMA((groups + phases,)),
            ],
            compiler_params=pltpu.CompilerParams(
                collective_id=0, has_side_effects=True, vmem_limit_bytes=60 * 1024 * 1024
            ),
        )(
            tile_counts,
            text_lengths,
            sample_image,
            cross_gate,
            text_rows,
            image_rows.reshape(samples * piece, vision),
            norm_gain,
            query_weight[0],
            keyval_weight[0, :, 0, :],
            output_weight[0],
        )
        return result[None]

    placed = (
        P("dp", "mp"),
        P("dp", ("phase", "mp"), None),
        P("dp"),
        P("dp"),
        P("dp"),
        P("phase", None),
        P("phase", "dp", "mp"),
        P("phase", None, "mp", None),
        P("phase", "dp", "mp"),
        P("phase"),
    )
    return jax.shard_map(
        on_device, mesh=mesh, in_specs=placed, out_specs=P("phase", "dp", "mp"), check_vma=False
    )
```
